32 devices in a mesh: kpt: 2 (over x), orb: 16 (over z, y, core).
Axes of the slice: x: 2, y: 2, z: 4, core: 2. Of those that a mesh axis runs over, the one named last changes fastest.
Arguments:
- wavefunctions: float32 [2, 48, 102400], P('kpt', 'orb'), may hold values from -8 to 8
- kpoint_vector: float32 [2, 3], P('kpt'), may hold values from -1 to 1
- kpoint_weight: float32 [2], P('kpt'), may hold values from 0.05 to 0.3
- occupation: float32 [48], replicated, may hold values from 0.25 to 2
- orbital_slot: int32 [48], replicated, may hold values from 0 to 47, as said below
- piece_rows: int32 [16], replicated, may hold values from 1 to 80, 640 in all
- external_potential: float32 [8, 6400], P(None, 'orb'), may hold values from -6 to 6
- core_density: float32 [8, 6400], P(None, 'orb'), may hold values from 0.1 to 4
Outputs:
- density: float32 [8, 6400], P(None, 'orb')
- new_orbitals: float32 [2, 48, 204800], P('kpt', None, 'orb')
The draws below stay inside these ranges and needn't reach their ends.
Inputs may be any that keep to these rules, and one draw needn't show every extreme that they name: `orbital_slot`: distinct slot numbers; 0 and 47 are always among them. `piece_rows`: the entries sum to 640.
All inputs are finite; a program needn't handle non-finite values.
Results may differ from the reference program's by a relative error of at most 0.00013.
Values sent between devices are 32-bit elements; how exact they have to be, the bound alone decides.
A program may use at most 64 MiB of HBM per device.

```python
import math
import jax
import jax.numpy as jnp
import numpy as np
from jax import lax

NX = 80
NY = 80
NZ = 8
ORB = 48
KPT = 2
SLOT_ALL = 48
ROWS = 640
CMAX = 80
N_ORB = 16


def draw_wavefunctions(key, part):
    noise_key, common_key, mixing_key, row_key, slot_key = jax.random.split(key, 5)
    array_shape = (KPT, SLOT_ALL, ROWS, 2 * NX)
    noise_part = jnp.clip(jax.random.normal(noise_key, array_shape, jnp.float32), -4.0, 4.0)
    common = jnp.clip(jax.random.normal(common_key, (KPT, 4, 1, ROWS, 2 * NX), jnp.float32), -4.0, 4.0)
    mixing = jax.random.uniform(mixing_key, (KPT, 4, SLOT_ALL, 1, 1), jnp.float32, -1.0, 1.0)
    shared = mixing[:, 0] * common[:, 0]
    for member in range(1, 4):
        shared = shared + mixing[:, member] * common[:, member]
    row_scale = jnp.exp(jax.random.uniform(row_key, (1, 1, ROWS, 1), jnp.float32, -1.15, 1.15))
    slot_scale = jnp.exp(jax.random.uniform(slot_key, (KPT, SLOT_ALL, 1, 1), jnp.float32, -0.35, 0.35))
    values = (noise_part + 0.5 * shared) * row_scale * slot_scale / jnp.sqrt(jnp.float32(ORB))
    return values.reshape(KPT, SLOT_ALL, ROWS * 2 * NX)


def draw_orbital_slot(key, part):
    first_key, second_key = jax.random.split(key)
    middle = jax.random.permutation(first_key, SLOT_ALL - 2)[:ORB - 2].astype(jnp.int32) + 1
    chosen = jnp.concatenate([jnp.zeros((1,), jnp.int32), middle, jnp.full((1,), SLOT_ALL - 1, jnp.int32)])
    return jax.random.permutation(second_key, chosen).astype(jnp.int32)


def levels(stream_key, shape, cuts, low, top_value):
    factor_of, own = 1.0, jax.random.fold_in(stream_key, 6)
    for position, blocks in cuts:
        heights = jnp.exp(jax.random.uniform(jax.random.fold_in(own, position), (blocks,), jnp.float32, low / len(cuts), top_value / len(cuts)))
        factor_of = factor_of * jnp.repeat(heights, shape[position] // blocks).reshape([-1 if axis == position else 1 for axis in range(len(shape))])
    return factor_of


def split_up(amount, total, reach, slope):
    loads = [(1 << 20) // math.isqrt(grade ** slope) + 1 for grade in range(2, amount + 1)]
    spare, given = total - reach - (amount - 1), [1] * (amount - 1)
    while spare > 0:
        movable = [i for i in range(amount - 1) if given[i] < reach]
        mass, left = sum([loads[i] for i in movable]), spare
        for i in movable:
            addition = min(reach - given[i], max(1, left * loads[i] // mass), spare)
            given[i] = given[i] + addition
            spare = spare - addition
    return np.array([reach] + given)


def uneven(key, count, total, most, skew):
    if count == 2:
        one = jax.random.randint(key, (), max(1, total - most), min(most, total - 1) + 1)
        return jnp.stack([one, total - one])
    tallies = jnp.asarray(split_up(count, total, most, skew), jnp.int32)
    twos = (count - 1) // 2
    giver, sink = tallies[1:1 + 2 * twos:2], tallies[2:2 + 2 * twos:2]
    margin = jnp.minimum(giver - 1, most - sink)
    shifted = jax.random.randint(jax.random.fold_in(key, 1), (twos,), 0, 1 << 20) % (margin + 1)
    tallies = tallies.at[1:1 + 2 * twos:2].set(giver - shifted).at[2:2 + 2 * twos:2].set(sink + shifted)
    return tallies[jax.random.permutation(jax.random.fold_in(key, 2), count)]


def normal_values(own_key, dims, width, reach, cuts=(), kind=jnp.bfloat16):
    values = width * jax.random.normal(own_key, dims, jnp.float32)
    if cuts:
        values = values * levels(own_key, dims, cuts, -0.22, 0.18)
    return jnp.clip(values, -reach, reach).astype(kind)


def setup_inputs(seed: int = 0) -> dict:
    splits = jax.random.split(jax.random.key(seed), 9)
    wavefunctions = draw_wavefunctions(jax.random.fold_in(splits[8], 71), 0)
    kpoint_vector = jnp.clip(jax.random.uniform(splits[1], (KPT, 3), jnp.float32, -1.0, 1.0) * levels(splits[1], (KPT, 3), ((0, 2),), -0.4, 0.0), -1.0, 1.0)
    kpoint_weight = jnp.clip(jnp.exp(math.log(0.3) - 1.7917595 * jax.random.uniform(splits[2], (KPT,), jnp.float32) ** levels(splits[2], (KPT,), ((0, 2),), -0.2, 0.2)), 0.05, 0.3)
    occupation = jnp.clip(jnp.exp(jax.random.uniform(splits[3], (ORB,), jnp.float32, math.log(0.25), math.log(2.0))), 0.25, 2.0)
    orbital_slot = draw_orbital_slot(jax.random.fold_in(splits[8], 71), 0)
    piece_rows = uneven(splits[5], N_ORB, ROWS, CMAX, 2).astype(jnp.int32)
    external_potential = normal_values(splits[6], (NZ, NY * NX), 1.5, 6.0, ((1, 16),), jnp.float32)
    core_density = jnp.clip(jnp.exp(math.log(4.0) - 3.6888794 * jax.random.uniform(splits[7], (NZ, NY * NX), jnp.float32) ** levels(splits[7], (NZ, NY * NX), ((1, 16),), -0.2, 0.2)), 0.1, 4.0)
    return {"wavefunctions": wavefunctions, "kpoint_vector": kpoint_vector, "kpoint_weight": kpoint_weight, "occupation": occupation, "orbital_slot": orbital_slot, "piece_rows": piece_rows, "external_potential": external_potential, "core_density": core_density}


magic_taps = (8.433424733352934e-07, -1.290557201342061e-05, 8.76298447621056e-05, -0.00030158038132690465, 0.001747237136729939, -0.009420470302010804, 0.023738214637249424, 0.0612625895831208, 0.9940415697834004, -0.06048952891969835, -0.021030251609303816, 0.013372634148547948, -0.0034412814449349387, 0.0004944322768868992, -5.185986881173433e-05, 2.7273449291197967e-06)
grid_step = 0.9
half_order = 14
spectrum_center = 13.0
spectrum_half = 17.0
exchange_coef = (3.0 / math.pi) ** (1.0 / 3.0)
exact_mode = lax.Precision.HIGHEST

def stencil_taps():
    factorial = math.factorial
    second_taps = {}
    first_taps = {}
    running = 0.0
    for offset in range(1, half_order + 1):
        weight_j = factorial(half_order) ** 2 / (factorial(half_order - offset) * factorial(half_order + offset))
        tap_sign = (-1.0) ** (offset + 1)
        second_taps[offset] = 2.0 * tap_sign * weight_j / offset ** 2
        second_taps[-offset] = second_taps[offset]
        first_taps[offset] = tap_sign * weight_j / offset
        first_taps[-offset] = -first_taps[offset]
        running = running + 2.0 * second_taps[offset]
    second_taps[0] = -running
    return (second_taps, first_taps)

def band_matrix(length, taps):
    matrix = np.zeros((length, length))
    for offset, tap_value in taps.items():
        matrix = matrix + tap_value * np.eye(length, k=offset)
    return matrix

def axis_tables(length):
    second_taps, first_taps = stencil_taps()
    magic_band = band_matrix(length, {tap_index - 8: magic_taps[tap_index] for tap_index in range(16)})
    return (band_matrix(length, second_taps) * (-0.5 / grid_step ** 2), band_matrix(length, first_taps) / grid_step, magic_band)

def apply_last(grid_field, matrix):
    return jnp.einsum('azyc,dc->azyd', grid_field, matrix, precision=exact_mode)

def apply_rows(grid_field, matrix):
    return jnp.einsum('wy,azyc->azwc', matrix, grid_field, precision=exact_mode)

def apply_planes(grid_field, matrix):
    return jnp.einsum('vz,azyc->avyc', matrix, grid_field, precision=exact_mode)

def swap_halves(values):
    half_width = values.shape[-1] // 2
    return jnp.concatenate([values[..., half_width:], -values[..., :half_width]], axis=-1)

def magic_tables(grid_field):
    half_width = grid_field.shape[3] // 2
    magic_x = jnp.asarray(np.kron(np.eye(2), axis_tables(half_width)[2]), jnp.float32)
    magic_y = jnp.asarray(axis_tables(grid_field.shape[2])[2], jnp.float32)
    magic_z = jnp.asarray(axis_tables(grid_field.shape[1])[2], jnp.float32)
    return (magic_x, magic_y, magic_z)

def magic_forward(grid_field):
    magic_x, magic_y, magic_z = magic_tables(grid_field)
    smooth = apply_last(grid_field, magic_x)
    smooth = apply_rows(smooth, magic_y)
    return apply_planes(smooth, magic_z)

def magic_backward(grid_field):
    magic_x, magic_y, magic_z = magic_tables(grid_field)
    coarse = apply_planes(grid_field, magic_z.T)
    coarse = apply_rows(coarse, magic_y.T)
    return apply_last(coarse, magic_x.T)

def kinetic(grid_field, wave_vector):
    half_width = grid_field.shape[3] // 2
    tables_x = axis_tables(half_width)
    tables_y = axis_tables(grid_field.shape[2])
    tables_z = axis_tables(grid_field.shape[1])
    twist_table = np.array([[0.0, 1.0], [-1.0, 0.0]])
    along_x = jnp.asarray(np.kron(np.eye(2), tables_x[0]), jnp.float32)
    along_x = along_x + wave_vector[0] * jnp.asarray(np.kron(twist_table, tables_x[1]), jnp.float32)
    along_x = along_x + 0.5 * jnp.sum(wave_vector * wave_vector) * jnp.eye(2 * half_width, dtype=jnp.float32)
    stack_y = jnp.stack([jnp.asarray(tables_y[0], jnp.float32), wave_vector[1] * jnp.asarray(tables_y[1], jnp.float32)])
    stack_z = jnp.stack([jnp.asarray(tables_z[0], jnp.float32), wave_vector[2] * jnp.asarray(tables_z[1], jnp.float32)])
    parts_y = jnp.einsum('swy,azyc->sazwc', stack_y, grid_field, precision=exact_mode)
    parts_z = jnp.einsum('svz,azyc->savyc', stack_z, grid_field, precision=exact_mode)
    return apply_last(grid_field, along_x) + parts_y[0] + parts_z[0] + swap_halves(parts_y[1] + parts_z[1])

def potential_pair(potential, planes, rows_y):
    shaped = potential.reshape(planes, rows_y, -1)
    return jnp.concatenate([shaped, shaped], axis=-1)

def chebyshev_image(grid_field, smooth, pair_field, wave_vector):
    applied = kinetic(grid_field, wave_vector) + magic_backward(pair_field[None] * smooth)
    first_term = (applied - spectrum_center * grid_field) / spectrum_half
    applied_again = kinetic(first_term, wave_vector) + magic_backward(pair_field[None] * magic_forward(first_term))
    return applied_again - spectrum_center * first_term

def split_stack(pieces):
    orbital_count, row_count, double_width = pieces.shape
    half_width = double_width // 2
    return pieces.reshape(orbital_count, row_count, 2, half_width).transpose(2, 0, 1, 3).reshape(2 * orbital_count, row_count * half_width)

def gram_of(stacked):
    return jnp.dot(stacked, stacked.T, precision=exact_mode, preferred_element_type=jnp.float32)

def rotate_with(gram_matrix, stacked, components, half_width):
    orbital_count = gram_matrix.shape[0] // 2
    gram_aa = gram_matrix[:orbital_count, :orbital_count]
    gram_ab = gram_matrix[:orbital_count, orbital_count:]
    gram_ba = gram_matrix[orbital_count:, :orbital_count]
    gram_bb = gram_matrix[orbital_count:, orbital_count:]
    over_real = gram_aa + gram_bb
    over_imag = gram_ab - gram_ba
    mean_square = jnp.trace(over_real) / (orbital_count * components) + 1e-06
    shrink_factor = 0.5 / (components * mean_square)
    rot_real = 1.5 * jnp.eye(orbital_count, dtype=jnp.float32) - shrink_factor * over_real
    rot_imag = -shrink_factor * over_imag
    rotation = jnp.concatenate([jnp.concatenate([rot_real, rot_imag], 1), jnp.concatenate([-rot_imag, rot_real], 1)], 0)
    new_stack = jnp.dot(rotation.T, stacked, precision=exact_mode, preferred_element_type=jnp.float32) / jnp.sqrt(mean_square)
    row_count = stacked.shape[1] // half_width
    return new_stack.reshape(2, orbital_count, row_count, half_width).transpose(1, 2, 0, 3).reshape(orbital_count, row_count, 2 * half_width)

def reference(wavefunctions, kpoint_vector, kpoint_weight, occupation, orbital_slot, piece_rows, external_potential, core_density):
    orbitals = jnp.take(wavefunctions, orbital_slot, axis=1).reshape(KPT, ORB, NZ, NY, 2 * NX)

    def density_term(inputs):
        grid_field, weight = inputs
        smooth = magic_forward(grid_field)
        squares = smooth[..., :NX] ** 2 + smooth[..., NX:] ** 2
        return weight * lax.optimization_barrier(jnp.sum(occupation[:, None, None, None] * squares, axis=0))
    density_terms = lax.map(density_term, (orbitals, kpoint_weight))
    density = lax.optimization_barrier(jnp.sum(density_terms, axis=0)).reshape(NZ, NY * NX)
    potential = external_potential - exchange_coef * jnp.power(density + core_density, 1.0 / 3.0)
    pair_field = potential_pair(potential, NZ, NY)
    offsets = (jnp.cumsum(piece_rows) - piece_rows).astype(jnp.int32)
    positions = offsets[:, None] + jnp.arange(CMAX, dtype=jnp.int32)[None, :]
    flat_index = jnp.minimum(positions, ROWS - 1).reshape(-1).astype(jnp.int32)
    flat_valid = (jnp.arange(CMAX, dtype=jnp.int32)[None, :] < piece_rows[:, None]).reshape(-1)

    def wave_step(inputs):
        grid_field, wave_vector = inputs
        smooth = magic_forward(grid_field)
        image_field = chebyshev_image(grid_field, smooth, pair_field, wave_vector)
        filtered = (2.0 * image_field / spectrum_half - grid_field).reshape(ORB, ROWS, 2 * NX)
        stacked = split_stack(filtered)
        rotated = rotate_with(gram_of(stacked), stacked, ROWS * 2 * NX, NX)
        padded = jnp.take(rotated, flat_index, axis=1)
        return jnp.where(flat_valid[None, :, None], padded, 0.0).reshape(ORB, N_ORB * CMAX * 2 * NX)
    new_orbitals = lax.map(wave_step, (orbitals, kpoint_vector))
    return (density, new_orbitals)
```

```python
import functools
import math

import jax
import jax.numpy as jnp
import numpy as np
from jax import lax
from jax.experimental import pallas as pl
from jax.experimental.pallas import tpu as pltpu
from jax.sharding import PartitionSpec as P

NX = 80
NY = 80
NZ = 8


magic_taps = (
    8.433424733352934e-07,
    -1.290557201342061e-05,
    8.76298447621056e-05,
    -0.00030158038132690465,
    0.001747237136729939,
    -0.009420470302010804,
    0.023738214637249424,
    0.0612625895831208,
    0.9940415697834004,
    -0.06048952891969835,
    -0.021030251609303816,
    0.013372634148547948,
    -0.0034412814449349387,
    0.0004944322768868992,
    -5.185986881173433e-05,
    2.7273449291197967e-06,
)
grid_step = 0.9
half_order = 14
spectrum_center = 13.0
spectrum_half = 17.0
exchange_coef = (3.0 / math.pi) ** (1.0 / 3.0)
exact_mode = lax.Precision.HIGHEST


def stencil_taps():
    factorial = math.factorial
    second_taps = {}
    first_taps = {}
    running = 0.0
    for offset in range(1, half_order + 1):
        weight_j = factorial(half_order) ** 2 / (
            factorial(half_order - offset) * factorial(half_order + offset)
        )
        tap_sign = (-1.0) ** (offset + 1)
        second_taps[offset] = 2.0 * tap_sign * weight_j / offset**2
        second_taps[-offset] = second_taps[offset]
        first_taps[offset] = tap_sign * weight_j / offset
        first_taps[-offset] = -first_taps[offset]
        running = running + 2.0 * second_taps[offset]
    second_taps[0] = -running
    return (second_taps, first_taps)


def band_matrix(length, taps):
    matrix = np.zeros((length, length))
    for offset, tap_value in taps.items():
        matrix = matrix + tap_value * np.eye(length, k=offset)
    return matrix


def axis_tables(length):
    second_taps, first_taps = stencil_taps()
    magic_band = band_matrix(
        length, {tap_index - 8: magic_taps[tap_index] for tap_index in range(16)}
    )
    return (
        band_matrix(length, second_taps) * (-0.5 / grid_step**2),
        band_matrix(length, first_taps) / grid_step,
        magic_band,
    )


MESH = pl.DeviceIdType.MESH
BF = jnp.bfloat16
VMEM = pl.BlockSpec(memory_space=pltpu.VMEM)
SMEM = pl.BlockSpec(memory_space=pltpu.SMEM)


def split(x):
    high = x.astype(BF)
    return high, (x - high.astype(jnp.float32)).astype(BF)


def split_table(x):
    high = x.astype(BF)
    return high, (x - high.astype(np.float32)).astype(BF)


def dot(a, b):
    return lax.dot_general(a, b, (((1,), (0,)), ((), ())), preferred_element_type=jnp.float32)


def dot_nt(a, b):
    return lax.dot_general(a, b, (((1,), (1,)), ((), ())), preferred_element_type=jnp.float32)


def mm(ah, al, bh, bl):
    return dot(ah, bh) + dot(ah, bl) + dot(al, bh)


def swap_lanes(x, slots):
    parts = []
    for s in range(slots):
        parts += [x[:, (2 * s + 1) * NX:(2 * s + 2) * NX], -x[:, 2 * s * NX:(2 * s + 1) * NX]]
    return jnp.concatenate(parts, axis=1)


def put_split(refs, at, x):
    high, low = split(x)
    refs[0][at, :] = high
    refs[1][at, :] = low


def tables(slots, wave_vector):
    d2, d1, magic = axis_tables(NX)
    d2z, d1z, magic_z = axis_tables(NZ)
    d2y, d1y, magic_y = axis_tables(NY)
    f = lambda m: np.asarray(m, np.float32)
    wide = lambda m: f(np.tile(m, (1, NZ)))
    tall = lambda m: f(np.repeat(m, NY, axis=1))
    eye = np.eye(2 * slots)
    magic_x = split_table(f(np.kron(eye, magic.T)))
    magic_xt = split_table(f(np.kron(eye, magic)))
    twist = np.array([[0.0, 1.0], [-1.0, 0.0]])
    along_x = (
        jnp.asarray(f(np.kron(eye, d2.T)))
        + wave_vector[0] * jnp.asarray(f(np.kron(np.eye(slots), np.kron(twist, d1).T)))
        + 0.5 * jnp.sum(wave_vector * wave_vector) * jnp.eye(2 * slots * NX, dtype=jnp.float32)
    )
    first = [wide(magic_y), tall(magic_z)]
    second = [
        wide(magic_y.T), tall(magic_z.T),
        wide(d2y), tall(np.eye(NZ)), wide(np.eye(NY)), tall(d2z),
        wave_vector[1] * jnp.asarray(wide(d1y)), wave_vector[2] * jnp.asarray(tall(d1z)),
    ]
    return first, second, magic_x, magic_xt, along_x


def tiles_of(rows, tile, body):
    def step(t, carry):
        body(pl.ds(pl.multiple_of(t * tile, tile), tile))
        return carry

    lax.fori_loop(0, rows // tile, step, 0)


TILE = 320


def smooth_kernel(slots, v_ref, my, mz, mxh, mxl, w_ref, smooth_ref, part_ref, mh_out, ml_out,
                  th, tl, dens):
    rows = NZ * NY
    for z in range(NZ):
        block = my[...] * mz[z:z + 1, :]
        put_split((mh_out, ml_out), pl.ds(z * NY, NY), block)

    def along(at):
        vh, vl = split(v_ref[at, :])
        put_split((th, tl), at, mm(vh, vl, mxh[...], mxl[...]))

    tiles_of(rows, TILE, along)

    def across(at):
        s = mm(mh_out[at, :], ml_out[at, :], th[...], tl[...])
        smooth_ref[at, :] = s
        q = s * s * w_ref[...]
        total = q[:, :NX]
        for i in range(1, 2 * slots):
            total = total + q[:, i * NX:(i + 1) * NX]
        dens[at, :] = total

    tiles_of(rows, TILE, across)
    group = 8
    for g in range(NY // group):
        part_ref[:, g * group * NX:(g + 1) * group * NX] = jnp.concatenate(
            [dens[pl.ds(g * group + y, NZ, stride=NY), :] for y in range(group)], axis=1
        )


def density_kernel(kpts, ranks, part_ref, ext_ref, core_ref, dens_ref, pot_ref,
                   send1, recv1, send2, recv2, own_d, recv_d, s1, r1, s2, r2, s3, r3):
    k = lax.axis_index("kpt")
    o = lax.axis_index("orb")
    every = kpts * ranks
    me = k * ranks + o
    planes = NZ // kpts
    width = ext_ref.shape[1]
    barrier = pltpu.get_barrier_semaphore()

    def peer(i):
        d = lax.rem(me + i, every)
        return d, d // ranks, lax.rem(d, ranks)

    def greet(i, c):
        _, dk, do = peer(i)
        pl.semaphore_signal(barrier, inc=1, device_id=(dk, do), device_id_type=MESH)
        return c

    lax.fori_loop(1, every, greet, 0)
    for j in range(every):
        a, b = divmod(j, ranks)
        send1[j] = part_ref[a * planes:(a + 1) * planes, b * width:(b + 1) * width]
    pl.semaphore_wait(barrier, every - 1)

    def copy1(i):
        d, dk, do = peer(i)
        return pltpu.make_async_remote_copy(
            src_ref=send1.at[d], dst_ref=recv1.at[me], send_sem=s1.at[d], recv_sem=r1.at[me],
            device_id=(dk, do), device_id_type=MESH)

    def copy2(i):
        d, dk, do = peer(i)
        return pltpu.make_async_remote_copy(
            src_ref=send2, dst_ref=recv2.at[me], send_sem=s2.at[d], recv_sem=r2.at[me],
            device_id=(dk, do), device_id_type=MESH)

    def copy3(i):
        dk = lax.rem(k + i, kpts)
        return pltpu.make_async_remote_copy(
            src_ref=own_d, dst_ref=recv_d.at[k], send_sem=s3.at[dk], recv_sem=r3.at[k],
            device_id=(dk, o), device_id_type=MESH)

    def arrived(i, buf, sends, recvs):
        d, dk, do = peer(i)
        return pltpu.make_async_remote_copy(
            src_ref=buf.at[d], dst_ref=buf.at[d], send_sem=sends.at[d], recv_sem=recvs.at[d],
            device_id=(dk, do), device_id_type=MESH)

    def loop(f):
        def step(i, c):
            f(i)
            return c
        lax.fori_loop(1, every, step, 0)

    loop(lambda i: copy1(i).start())
    recv1[me] = send1[me]
    loop(lambda i: arrived(i, recv1, s1, r1).wait_recv())
    total = recv1[0]
    for j in range(1, every):
        total = total + recv1[j]
    own_d[...] = total
    recv_d[k] = total

    def own_planes(ref):
        picked = ref[:planes, :]
        for a in range(1, kpts):
            picked = jnp.where(k == a, ref[a * planes:(a + 1) * planes, :], picked)
        return picked

    level = total + own_planes(core_ref)
    value = own_planes(ext_ref) - exchange_coef * jnp.exp(jnp.log(level) * (1.0 / 3.0))
    send2[...] = value
    recv2[me] = value
    loop(lambda i: copy2(i).start())
    for i in range(1, kpts):
        copy3(i).start()
    loop(lambda i: arrived(i, recv2, s2, r2).wait_recv())
    for j in range(every):
        a, b = divmod(j, ranks)
        pot_ref[a * planes:(a + 1) * planes, b * width:(b + 1) * width] = recv2[j]
    for i in range(1, kpts):
        dk = lax.rem(k + i, kpts)
        pltpu.make_async_remote_copy(
            src_ref=own_d, dst_ref=recv_d.at[dk], send_sem=s3.at[dk], recv_sem=r3.at[dk],
            device_id=(dk, o), device_id_type=MESH).wait_recv()
    for a in range(kpts):
        dens_ref[a * planes:(a + 1) * planes, :] = recv_d[a]
    loop(lambda i: copy1(i).wait_send())
    loop(lambda i: copy2(i).wait_send())
    for i in range(1, kpts):
        copy3(i).wait_send()


def filter_kernel(slots, v_ref, smooth_ref, pot_ref, mh, ml, ty, tz, a1, b1, a2, b2, dy, dz,
                  mxh, mxl, mxth, mxtl, kx_ref, out_ref,
                  kxh, kxl, pair, first, vh, vl, jh, jl, ph, plo, wh, wl, nh, nl, ah, al, dh, dl):
    rows = NZ * NY
    for z in range(NZ):
        at = pl.ds(z * NY, NY)
        put_split((nh, nl), at, ty[...] * tz[z:z + 1, :])
        put_split((ah, al), at, a1[...] * b1[z:z + 1, :] + a2[...] * b2[z:z + 1, :])
        put_split((dh, dl), at, dy[...] * b1[z:z + 1, :] + a2[...] * dz[z:z + 1, :])
    kxh[...], kxl[...] = split(kx_ref[...])
    for y in range(NY):
        line = pot_ref[:, y * NX:(y + 1) * NX]
        pair[pl.ds(y, NZ, stride=NY), :] = line

    def wide_pair(at):
        return jnp.concatenate([pair[at, :]] * (2 * slots), axis=1)

    def prepare(at):
        high, low = split(v_ref[at, :])
        vh[at, :] = high
        vl[at, :] = low
        put_split((jh, jl), at, swap_lanes(v_ref[at, :], slots))
        put_split((ph, plo), at, smooth_ref[at, :] * wide_pair(at))

    tiles_of(rows, 160, prepare)

    def back(at):
        put_split((wh, wl), at, mm(nh[at, :], nl[at, :], ph[...], plo[...]))

    def kinetic_of(at):
        return (
            mm(vh[at, :], vl[at, :], kxh[...], kxl[...])
            + mm(wh[at, :], wl[at, :], mxth[...], mxtl[...])
            + mm(ah[at, :], al[at, :], vh[...], vl[...])
            + mm(dh[at, :], dl[at, :], jh[...], jl[...])
        )

    tiles_of(rows, TILE, back)

    def apply_first(at):
        first[at, :] = (kinetic_of(at) - spectrum_center * v_ref[at, :]) * (1.0 / spectrum_half)

    tiles_of(rows, TILE, apply_first)

    def prepare_again(at):
        x = first[at, :]
        high, low = split(x)
        vh[at, :] = high
        vl[at, :] = low
        put_split((jh, jl), at, swap_lanes(x, slots))
        put_split((wh, wl), at, mm(high, low, mxh[...], mxl[...]))

    tiles_of(rows, TILE, prepare_again)

    def smooth_again(at):
        s = mm(mh[at, :], ml[at, :], wh[...], wl[...])
        put_split((ph, plo), at, s * wide_pair(at))

    tiles_of(rows, TILE, smooth_again)
    tiles_of(rows, TILE, back)

    def finish(at):
        image = kinetic_of(at) - spectrum_center * first[at, :]
        out_ref[at, :] = (2.0 / spectrum_half) * image - v_ref[at, :]

    tiles_of(rows, TILE, finish)


def exchange_kernel(slots, ranks, cap, orbs, f_ref, off_ref, rows_ref, pick_ref, out_ref,
                    padded, send, recv, flat, gsend, grecv, s1, r1, s2, r2):
    o = lax.axis_index("orb")
    k = lax.axis_index("kpt")
    rows = NZ * NY
    count = slots * ranks
    barrier = pltpu.get_barrier_semaphore()

    def loop(f):
        def step(i, c):
            f(i)
            return c
        lax.fori_loop(1, ranks, step, 0)

    def peer(i):
        return lax.rem(o + i, ranks)

    loop(lambda i: pl.semaphore_signal(barrier, inc=1, device_id=(k, peer(i)), device_id_type=MESH))
    width = f_ref.shape[1]
    lane_tiles = -(-width // 128)
    block = lane_tiles * cap
    height = padded.shape[0] // lane_tiles
    for t in range(lane_tiles):
        used_lanes = min(128, width - t * 128)
        if used_lanes < 128:
            padded[t * height:t * height + rows, :] = jnp.zeros((rows, 128), jnp.float32)
        padded[t * height:t * height + rows, :used_lanes] = f_ref[:, t * 128:t * 128 + used_lanes]
        padded[t * height + rows:(t + 1) * height, :] = jnp.zeros((height - rows, 128), jnp.float32)

    def block_of(ref, d):
        return ref.at[pl.ds(pl.multiple_of(d * block, 8), block)]

    def put_window(ref, d):
        for t in range(lane_tiles):
            ref[pl.ds(d * block + t * cap, cap), :] = padded[pl.ds(off_ref[d] + t * height, cap), :]

    pl.semaphore_wait(barrier, ranks - 1)

    def copy(i, src, dst, sends, recvs):
        d = peer(i)
        return pltpu.make_async_remote_copy(
            src_ref=src(d), dst_ref=dst(o), send_sem=sends.at[d], recv_sem=recvs.at[o],
            device_id=(k, d), device_id_type=MESH)

    def arrived(i, dst, sends, recvs):
        d = peer(i)
        return pltpu.make_async_remote_copy(
            src_ref=dst(d), dst_ref=dst(d), send_sem=sends.at[d], recv_sem=recvs.at[d],
            device_id=(k, d), device_id_type=MESH)

    send_at = functools.partial(block_of, send)
    recv_at = functools.partial(block_of, recv)

    def gram_at(d):
        return grecv.at[d]

    def push(i):
        put_window(send, peer(i))
        copy(i, send_at, recv_at, s1, r1).start()

    loop(push)
    put_window(recv, o)
    loop(lambda i: arrived(i, recv_at, s1, r1).wait_recv())
    live = rows_ref[o]
    group = 4
    span = group * 2 * NX
    lane = lax.broadcasted_iota(jnp.int32, (count, span), 1)
    is_real = lax.rem(lane, 2 * NX) < NX

    def turned(x):
        return jnp.where(is_real, pltpu.roll(x, span - NX, 1), -pltpu.roll(x, NX, 1))

    def build(g, carry):
        real, imag = carry
        lines = []
        for j in range(group):
            r = g * group + j
            x3 = jnp.concatenate(
                [recv[pl.ds(t * cap + r, ranks, stride=block), :] for t in range(lane_tiles)], axis=1
            )
            line = jnp.concatenate([x3[:, s * 2 * NX:(s + 1) * 2 * NX] for s in range(slots)], axis=0)
            lines.append(line)
        x = jnp.concatenate(lines, axis=1)
        x = jnp.where(lane // (2 * NX) + g * group < live, x, 0.0)
        flat[:, pl.ds(pl.multiple_of(g * span, 128), span)] = x
        xh, xl = split(x)
        th, tl = split(turned(x))
        real = real + dot_nt(xh, xh) + dot_nt(xh, xl) + dot_nt(xl, xh)
        imag = imag + dot_nt(xh, th) + dot_nt(xh, tl) + dot_nt(xl, th)
        return real, imag

    zero = jnp.zeros((count, count), jnp.float32)
    real, imag = lax.fori_loop(0, cap // group, build, (zero, zero))
    ri = lax.broadcasted_iota(jnp.int32, (count, count), 0)
    ci = lax.broadcasted_iota(jnp.int32, (count, count), 1)
    packed = jnp.where(ri <= ci, real, imag)
    half = count // 2
    mine = jnp.concatenate([packed[:half], packed[half:]], axis=1)
    gsend[...] = mine
    grecv[o] = mine
    loop(lambda i: copy(i, lambda d: gsend, gram_at, s2, r2).start())
    loop(lambda i: arrived(i, gram_at, s2, r2).wait_recv())
    total = grecv[0]
    for j in range(1, ranks):
        total = total + grecv[j]
    packed = jnp.concatenate([total[:, :count], total[:, count:]], axis=0)
    other = packed.T
    real = jnp.where(ri <= ci, packed, other)
    imag = jnp.where(ri > ci, packed, jnp.where(ri < ci, -other, 0.0))
    pick = pick_ref[...]
    exact = functools.partial(jnp.dot, precision=exact_mode, preferred_element_type=jnp.float32)
    real_picked = exact(pick, real)
    imag_picked = exact(pick, imag)
    diagonal = jnp.sum(jnp.where(ri == ci, real, 0.0), axis=1, keepdims=True)
    trace = jnp.sum(exact(pick, jnp.broadcast_to(diagonal, (count, 128)))[:, :1])
    components = rows * 2 * NX
    mean_square = trace / (orbs * components) + 1e-06
    shrink = 0.5 / (components * mean_square)
    norm = 1.0 / jnp.sqrt(jnp.full((1, 1), mean_square, jnp.float32))
    used = jnp.sum(pick, axis=0, keepdims=True)
    rot_real = (1.5 * pick - shrink * real_picked * used) * norm
    rot_imag = (shrink * imag_picked * used) * norm
    rh, rl = split(rot_real)
    ih, il = split(rot_imag)

    def rotate(g, c):
        at = pl.ds(pl.multiple_of(g * span, 128), span)
        x = flat[:, at]
        xh, xl = split(x)
        th, tl = split(turned(x))
        out_ref[:, at] = mm(rh, rl, xh, xl) - mm(ih, il, th, tl)
        return c

    lax.fori_loop(0, cap // group, rotate, 0)
    loop(lambda i: copy(i, send_at, recv_at, s1, r1).wait_send())
    loop(lambda i: copy(i, lambda d: gsend, gram_at, s2, r2).wait_send())


def on_device(wavefunctions, kpoint_vector, kpoint_weight, occupation, orbital_slot, piece_rows,
              external_potential, core_density):
    f32 = jnp.float32
    slots = wavefunctions.shape[1]
    ranks = lax.axis_size("orb")
    kpts = lax.axis_size("kpt")
    own = lax.axis_index("orb")
    orbs = orbital_slot.shape[0]
    rows = NZ * NY
    cap = 2 * rows // ranks
    width = slots * 2 * NX
    slab = external_potential.shape[1]
    v = wavefunctions[0].reshape(slots, rows, 2 * NX).transpose(1, 0, 2).reshape(rows, width)
    wave_vector = kpoint_vector[0]
    offsets = jnp.cumsum(piece_rows) - piece_rows
    slot_ids = own * slots + jnp.arange(slots, dtype=jnp.int32)
    matches = (orbital_slot[:, None] == slot_ids[None, :]).astype(f32)
    weights = kpoint_weight[0] * jnp.sum(matches * occupation[:, None], axis=0)
    weights = jnp.repeat(weights, 2 * NX)[None, :]
    place = (orbital_slot % slots) * ranks + orbital_slot // slots
    pick = (place[:, None] == jnp.arange(slots * ranks, dtype=jnp.int32)[None, :]).astype(f32)
    first, second, mx, mxt, kx = tables(slots, wave_vector)
    sds = jax.ShapeDtypeStruct
    big = lambda n, w: [pltpu.VMEM((rows, w), BF)] * n
    dma = pltpu.SemaphoreType.DMA
    smooth, part, mh, ml = pl.pallas_call(
        functools.partial(smooth_kernel, slots),
        out_shape=[sds((rows, width), f32), sds((NZ, NY * NX), f32), sds((rows, rows), BF),
                   sds((rows, rows), BF)],
        in_specs=[VMEM] * 6, out_specs=[VMEM] * 4,
        scratch_shapes=big(2, width) + [pltpu.VMEM((rows, NX), f32)],
        name="smooth",
    )(v, *first, *mx, weights)
    every = kpts * ranks
    planes = NZ // kpts
    density, potential = pl.pallas_call(
        functools.partial(density_kernel, kpts, ranks),
        out_shape=[sds((NZ, slab), f32), sds((NZ, NY * NX), f32)],
        in_specs=[VMEM] * 3, out_specs=[VMEM] * 2,
        scratch_shapes=[pltpu.VMEM((every, planes, slab), f32)] * 2
        + [pltpu.VMEM((planes, slab), f32), pltpu.VMEM((every, planes, slab), f32),
           pltpu.VMEM((planes, slab), f32), pltpu.VMEM((kpts, planes, slab), f32)]
        + [dma((every,))] * 4 + [dma((kpts,))] * 2,
        compiler_params=pltpu.CompilerParams(collective_id=0, has_side_effects=True),
        name="density",
    )(part, external_potential, core_density)
    filtered = pl.pallas_call(
        functools.partial(filter_kernel, slots),
        out_shape=sds((rows, width), f32),
        in_specs=[VMEM] * 18, out_specs=VMEM,
        scratch_shapes=[pltpu.VMEM((width, width), BF)] * 2 + [pltpu.VMEM((rows, NX), f32), pltpu.VMEM((rows, width), f32)]
        + big(8, width) + big(6, rows),
        name="filter",
    )(v, smooth, potential, mh, ml, *second, *mx, *mxt, kx)
    count = slots * ranks
    lane_tiles = -(-width // 128)
    new_rows = pl.pallas_call(
        functools.partial(exchange_kernel, slots, ranks, cap, orbs),
        out_shape=sds((orbs, cap * 2 * NX), f32),
        in_specs=[VMEM, SMEM, SMEM, VMEM], out_specs=VMEM,
        scratch_shapes=[pltpu.VMEM((lane_tiles * (rows + (cap + 15) // 8 * 8), 128), f32)]
        + [pltpu.VMEM((ranks * lane_tiles * cap, 128), f32)] * 2
        + [pltpu.VMEM((count, cap * 2 * NX), f32), pltpu.VMEM((count // 2, 2 * count), f32),
           pltpu.VMEM((ranks, count // 2, 2 * count), f32)] + [dma((ranks,))] * 4,
        compiler_params=pltpu.CompilerParams(collective_id=1, has_side_effects=True),
        name="exchange",
    )(filtered, offsets, piece_rows, pick)
    return (density, new_rows[None])


def solution(mesh):
    in_specs = (
        P("kpt", "orb", None),
        P("kpt", None),
        P("kpt"),
        P(),
        P(),
        P(),
        P(None, "orb"),
        P(None, "orb"),
    )
    out_specs = (P(None, "orb"), P("kpt", None, "orb"))
    return jax.shard_map(
        on_device, mesh=mesh, in_specs=in_specs, out_specs=out_specs, check_vma=False
    )
```

```python
import functools
import math

import jax
import jax.numpy as jnp
import numpy as np
from jax import lax
from jax.experimental import pallas as pl
from jax.experimental.pallas import tpu as pltpu
from jax.sharding import PartitionSpec as P

NX = 80
NY = 80
NZ = 8


magic_taps = (
    8.433424733352934e-07,
    -1.290557201342061e-05,
    8.76298447621056e-05,
    -0.00030158038132690465,
    0.001747237136729939,
    -0.009420470302010804,
    0.023738214637249424,
    0.0612625895831208,
    0.9940415697834004,
    -0.06048952891969835,
    -0.021030251609303816,
    0.013372634148547948,
    -0.0034412814449349387,
    0.0004944322768868992,
    -5.185986881173433e-05,
    2.7273449291197967e-06,
)
grid_step = 0.9
half_order = 14
spectrum_center = 13.0
spectrum_half = 17.0
exchange_coef = (3.0 / math.pi) ** (1.0 / 3.0)
exact_mode = lax.Precision.HIGHEST


def stencil_taps():
    factorial = math.factorial
    second_taps = {}
    first_taps = {}
    running = 0.0
    for offset in range(1, half_order + 1):
        weight_j = factorial(half_order) ** 2 / (
            factorial(half_order - offset) * factorial(half_order + offset)
        )
        tap_sign = (-1.0) ** (offset + 1)
        second_taps[offset] = 2.0 * tap_sign * weight_j / offset**2
        second_taps[-offset] = second_taps[offset]
        first_taps[offset] = tap_sign * weight_j / offset
        first_taps[-offset] = -first_taps[offset]
        running = running + 2.0 * second_taps[offset]
    second_taps[0] = -running
    return (second_taps, first_taps)


def band_matrix(length, taps):
    matrix = np.zeros((length, length))
    for offset, tap_value in taps.items():
        matrix = matrix + tap_value * np.eye(length, k=offset)
    return matrix


def axis_tables(length):
    second_taps, first_taps = stencil_taps()
    magic_band = band_matrix(
        length, {tap_index - 8: magic_taps[tap_index] for tap_index in range(16)}
    )
    return (
        band_matrix(length, second_taps) * (-0.5 / grid_step**2),
        band_matrix(length, first_taps) / grid_step,
        magic_band,
    )


MESH = pl.DeviceIdType.MESH
BF = jnp.bfloat16
VMEM = pl.BlockSpec(memory_space=pltpu.VMEM)
SMEM = pl.BlockSpec(memory_space=pltpu.SMEM)


def split(x):
    high = x.astype(BF)
    return high, (x - high.astype(jnp.float32)).astype(BF)


def dot(a, b):
    return lax.dot_general(a, b, (((1,), (0,)), ((), ())), preferred_element_type=jnp.float32)


def dot_nt(a, b):
    return lax.dot_general(a, b, (((1,), (1,)), ((), ())), preferred_element_type=jnp.float32)


def mm(ah, al, bh, bl):
    return dot(ah, bh) + dot(ah, bl) + dot(al, bh)


def swap_lanes(x, slots):
    parts = []
    for s in range(slots):
        parts += [x[:, (2 * s + 1) * NX:(2 * s + 2) * NX], -x[:, 2 * s * NX:(2 * s + 1) * NX]]
    return jnp.concatenate(parts, axis=1)


def put_split(refs, at, x):
    high, low = split(x)
    refs[0][at, :] = high
    refs[1][at, :] = low


def tables():
    d2, d1, magic = axis_tables(NX)
    d2z, d1z, magic_z = axis_tables(NZ)
    d2y, d1y, magic_y = axis_tables(NY)
    f = lambda m: np.asarray(m, np.float32)
    wide = lambda m: f(np.tile(m, (1, NZ)))
    tall = lambda m: f(np.repeat(m, NY, axis=1))
    pair = np.eye(2)
    twist = np.array([[0.0, 1.0], [-1.0, 0.0]])
    return [
        wide(magic_y), tall(magic_z), wide(magic_y.T), tall(magic_z.T),
        wide(d2y), tall(np.eye(NZ)), wide(np.eye(NY)), tall(d2z), wide(d1y), tall(d1z),
        f(np.kron(pair, magic.T)), f(np.kron(pair, magic)),
        f(np.kron(pair, d2.T)), f(np.kron(twist, d1).T),
    ]


def tiles_of(rows, tile, body):
    def step(t, carry):
        body(pl.ds(pl.multiple_of(t * tile, tile), tile))
        return carry

    lax.fori_loop(0, rows // tile, step, 0)


TILE = 320
CHUNKS = 5


def place_diagonal(refs, block, slots):
    size = block.shape[0]
    for n in range(slots):
        parts = [jnp.zeros((size, n * size), jnp.float32)] * (n > 0) + [block]
        if n < slots - 1:
            parts.append(jnp.zeros((size, (slots - 1 - n) * size), jnp.float32))
        put_split(refs, pl.ds(n * size, size), jnp.concatenate(parts, axis=1))


def field_kernel(slots, kpts, ranks, wf_ref, occ_ref, slot_ref, q_ref, kw_ref, ext_ref, core_ref,
                 my, mz, ty, tz, a1, b1, a2, b2, dy, dz, mx, mxt, kx0, kx1, dens_ref, out_ref,
                 vt, v_ref, smooth_ref, part_ref, dens, pot_ref, pair, first,
                 mh, ml, nh, nl, ah, al, dh, dl, mxh, mxl, mxth, mxtl, kxh, kxl,
                 vh, vl, jh, jl, ph, plo, wh, wl,
                 send1, recv1, send2, recv2, own_d, recv_d, s1, r1, s2, r2, s3, r3):
    rows = NZ * NY
    full = slots * 2 * NX
    k = lax.axis_index("kpt")
    o = lax.axis_index("orb")
    every = kpts * ranks
    me = k * ranks + o
    planes = NZ // kpts
    width = ext_ref.shape[1]
    barrier = pltpu.get_barrier_semaphore()

    def peer(i):
        d = lax.rem(me + i, every)
        return d, d // ranks, lax.rem(d, ranks)

    def greet(i, c):
        _, dk, do = peer(i)
        pl.semaphore_signal(barrier, inc=1, device_id=(dk, do), device_id_type=MESH)
        return c

    lax.fori_loop(1, every, greet, 0)

    gather = 4
    lines = gather * 2 * NX // 128
    groups = rows // gather
    lane_tiles = -(-full // 128)
    for m in range(gather):
        parts = []
        for n in range(slots):
            start, stop = m * 2 * NX, (m + 1) * 2 * NX
            while start < stop:
                j = start // 128
                end = min(stop, (j + 1) * 128)
                x = wf_ref[pl.ds(n * groups * lines + j, groups, stride=lines), :]
                parts.append(x[:, start - j * 128:end - j * 128])
                start = end
        if lane_tiles * 128 > full:
            parts.append(jnp.zeros((groups, lane_tiles * 128 - full), jnp.float32))
        x = jnp.concatenate(parts, axis=1)
        for t in range(lane_tiles):
            vt[pl.ds(t * rows + m, groups, stride=gather), :] = x[:, t * 128:(t + 1) * 128]
    for t in range(lane_tiles):
        used = min(128, full - t * 128)
        v_ref[:, t * 128:t * 128 + used] = vt[t * rows:(t + 1) * rows, :used]
    for z in range(NZ):
        put_split((mh, ml), pl.ds(z * NY, NY), my[...] * mz[z:z + 1, :])
    place_diagonal((mxh, mxl), mx[...], slots)
    loads = [
        kw_ref[0] * jnp.sum(jnp.where(slot_ref[...] == o * slots + n, occ_ref[...], 0.0), axis=1,
                            keepdims=True)
        for n in range(slots)
    ]

    def along(at):
        high, low = split(v_ref[at, :])
        vh[at, :] = high
        vl[at, :] = low
        put_split((wh, wl), at, mm(high, low, mxh[...], mxl[...]))

    tiles_of(rows, TILE, along)

    def across(at):
        x = mm(mh[at, :], ml[at, :], wh[...], wl[...])
        smooth_ref[at, :] = x
        total = jnp.zeros((TILE, NX), jnp.float32)
        for n in range(slots):
            re = x[:, 2 * n * NX:(2 * n + 1) * NX]
            im = x[:, (2 * n + 1) * NX:(2 * n + 2) * NX]
            total = total + loads[n] * (re * re + im * im)
        dens[at, :] = total

    tiles_of(rows, TILE, across)
    group = 8
    for g in range(NY // group):
        part_ref[:, g * group * NX:(g + 1) * group * NX] = jnp.concatenate(
            [dens[pl.ds(g * group + y, NZ, stride=NY), :] for y in range(group)], axis=1
        )
    for j in range(every):
        a, b = divmod(j, ranks)
        send1[j] = part_ref[a * planes:(a + 1) * planes, b * width:(b + 1) * width]
    pl.semaphore_wait(barrier, every - 1)

    def copy1(i):
        d, dk, do = peer(i)
        return pltpu.make_async_remote_copy(
            src_ref=send1.at[d], dst_ref=recv1.at[me], send_sem=s1.at[d], recv_sem=r1.at[me],
            device_id=(dk, do), device_id_type=MESH)

    def copy2(i):
        d, dk, do = peer(i)
        return pltpu.make_async_remote_copy(
            src_ref=send2, dst_ref=recv2.at[me], send_sem=s2.at[d], recv_sem=r2.at[me],
            device_id=(dk, do), device_id_type=MESH)

    def copy3(i):
        dk = lax.rem(k + i, kpts)
        return pltpu.make_async_remote_copy(
            src_ref=own_d, dst_ref=recv_d.at[k], send_sem=s3.at[dk], recv_sem=r3.at[k],
            device_id=(dk, o), device_id_type=MESH)

    def arrived(i, buf, sends, recvs):
        d, dk, do = peer(i)
        return pltpu.make_async_remote_copy(
            src_ref=buf.at[d], dst_ref=buf.at[d], send_sem=sends.at[d], recv_sem=recvs.at[d],
            device_id=(dk, do), device_id_type=MESH)

    def loop(f):
        def step(i, c):
            f(i)
            return c
        lax.fori_loop(1, every, step, 0)

    loop(lambda i: copy1(i).start())
    recv1[me] = send1[me]

    for z in range(NZ):
        at = pl.ds(z * NY, NY)
        put_split((nh, nl), at, ty[...] * tz[z:z + 1, :])
        put_split((ah, al), at, a1[...] * b1[z:z + 1, :] + a2[...] * b2[z:z + 1, :])
        put_split((dh, dl), at, dy[...] * (q_ref[0, 1] * b1[z:z + 1, :])
                  + a2[...] * (q_ref[0, 2] * dz[z:z + 1, :]))
    place_diagonal((mxth, mxtl), mxt[...], slots)
    half_q2 = 0.5 * (q_ref[0, 0] * q_ref[0, 0] + q_ref[0, 1] * q_ref[0, 1] + q_ref[0, 2] * q_ref[0, 2])
    eye = (lax.broadcasted_iota(jnp.int32, (2 * NX, 2 * NX), 0)
           == lax.broadcasted_iota(jnp.int32, (2 * NX, 2 * NX), 1))
    along_x = kx0[...] + q_ref[0, 0] * kx1[...] + jnp.where(eye, half_q2, 0.0)
    place_diagonal((kxh, kxl), along_x, slots)

    def twist(at):
        put_split((jh, jl), at, swap_lanes(v_ref[at, :], slots))

    tiles_of(rows, 160, twist)

    loop(lambda i: arrived(i, recv1, s1, r1).wait_recv())
    total = recv1[0]
    for j in range(1, every):
        total = total + recv1[j]
    own_d[...] = total
    recv_d[k] = total

    def own_planes(ref):
        picked = ref[:planes, :]
        for a in range(1, kpts):
            picked = jnp.where(k == a, ref[a * planes:(a + 1) * planes, :], picked)
        return picked

    level = total + own_planes(core_ref)
    value = own_planes(ext_ref) - exchange_coef * jnp.exp(jnp.log(level) * (1.0 / 3.0))
    send2[...] = value
    recv2[me] = value
    loop(lambda i: copy2(i).start())
    for i in range(1, kpts):
        copy3(i).start()

    def kinetic_of(at):
        return (
            mm(vh[at, :], vl[at, :], kxh[...], kxl[...])
            + mm(ah[at, :], al[at, :], vh[...], vl[...])
            + mm(dh[at, :], dl[at, :], jh[...], jl[...])
        )

    def begin(at):
        first[at, :] = kinetic_of(at) - spectrum_center * v_ref[at, :]

    tiles_of(rows, TILE, begin)
    loop(lambda i: arrived(i, recv2, s2, r2).wait_recv())
    for j in range(every):
        a, b = divmod(j, ranks)
        pot_ref[a * planes:(a + 1) * planes, b * width:(b + 1) * width] = recv2[j]
    for i in range(1, kpts):
        dk = lax.rem(k + i, kpts)
        pltpu.make_async_remote_copy(
            src_ref=own_d, dst_ref=recv_d.at[dk], send_sem=s3.at[dk], recv_sem=r3.at[dk],
            device_id=(dk, o), device_id_type=MESH).wait_recv()
    for a in range(kpts):
        dens_ref[a * planes:(a + 1) * planes, :] = recv_d[a]
    loop(lambda i: copy1(i).wait_send())
    loop(lambda i: copy2(i).wait_send())
    for i in range(1, kpts):
        copy3(i).wait_send()
    for y in range(NY):
        pair[pl.ds(y, NZ, stride=NY), :] = pot_ref[:, y * NX:(y + 1) * NX]

    def wide_pair(at):
        return jnp.concatenate([pair[at, :]] * (2 * slots), axis=1)

    def weigh(at):
        put_split((ph, plo), at, smooth_ref[at, :] * wide_pair(at))

    tiles_of(rows, 160, weigh)

    def back(at):
        put_split((wh, wl), at, mm(nh[at, :], nl[at, :], ph[...], plo[...]))

    def potential_of(at):
        return mm(wh[at, :], wl[at, :], mxth[...], mxtl[...])

    tiles_of(rows, TILE, back)

    def apply_first(at):
        x = (first[at, :] + potential_of(at)) * (1.0 / spectrum_half)
        first[at, :] = x
        high, low = split(x)
        vh[at, :] = high
        vl[at, :] = low
        put_split((jh, jl), at, swap_lanes(x, slots))

    tiles_of(rows, 160, apply_first)

    def prepare_again(at):
        put_split((wh, wl), at, mm(vh[at, :], vl[at, :], mxh[...], mxl[...]))

    tiles_of(rows, TILE, prepare_again)

    def smooth_again(at):
        put_split((ph, plo), at, mm(mh[at, :], ml[at, :], wh[...], wl[...]) * wide_pair(at))

    tiles_of(rows, TILE, smooth_again)
    tiles_of(rows, TILE, back)

    def finish(at):
        image = kinetic_of(at) + potential_of(at) - spectrum_center * first[at, :]
        out_ref[at, :] = (2.0 / spectrum_half) * image - v_ref[at, :]

    tiles_of(rows, TILE, finish)


def exchange_kernel(slots, ranks, cap, orbs, f_ref, off_ref, rows_ref, pick_ref, out_ref,
                    padded, send, recv, flat, gsend, grecv, s1, r1, s2, r2):
    o = lax.axis_index("orb")
    k = lax.axis_index("kpt")
    rows = NZ * NY
    count = slots * ranks
    barrier = pltpu.get_barrier_semaphore()

    def loop(f):
        def step(i, c):
            f(i)
            return c
        lax.fori_loop(1, ranks, step, 0)

    def peer(i):
        return lax.rem(o + i, ranks)

    loop(lambda i: pl.semaphore_signal(barrier, inc=1, device_id=(k, peer(i)), device_id_type=MESH))
    width = f_ref.shape[1]
    lane_tiles = -(-width // 128)
    parts = CHUNKS
    chunk = cap // parts
    block = lane_tiles * chunk
    height = padded.shape[0] // lane_tiles
    for t in range(lane_tiles):
        used_lanes = min(128, width - t * 128)
        if used_lanes < 128:
            padded[t * height:t * height + rows, :] = jnp.zeros((rows, 128), jnp.float32)
        padded[t * height:t * height + rows, :used_lanes] = f_ref[:, t * 128:t * 128 + used_lanes]
        padded[t * height + rows:(t + 1) * height, :] = jnp.zeros((height - rows, 128), jnp.float32)

    def block_of(ref, c, d):
        return ref.at[pl.ds(pl.multiple_of((c * ranks + d) * block, 8), block)]

    def put_window(ref, c, d):
        for t in range(lane_tiles):
            at = pl.ds((c * ranks + d) * block + t * chunk, chunk)
            ref[at, :] = padded[pl.ds(off_ref[d] + c * chunk + t * height, chunk), :]

    pl.semaphore_wait(barrier, ranks - 1)

    def chunk_copy(c, i):
        d = peer(i)
        return pltpu.make_async_remote_copy(
            src_ref=block_of(send, c, d), dst_ref=block_of(recv, c, o),
            send_sem=s1.at[c * ranks + d], recv_sem=r1.at[c * ranks + o],
            device_id=(k, d), device_id_type=MESH)

    def chunk_arrived(c, i):
        d = peer(i)
        return pltpu.make_async_remote_copy(
            src_ref=block_of(recv, c, d), dst_ref=block_of(recv, c, d),
            send_sem=s1.at[c * ranks + d], recv_sem=r1.at[c * ranks + d],
            device_id=(k, d), device_id_type=MESH)

    def copy(i):
        d = peer(i)
        return pltpu.make_async_remote_copy(
            src_ref=gsend, dst_ref=grecv.at[o], send_sem=s2.at[d], recv_sem=r2.at[o],
            device_id=(k, d), device_id_type=MESH)

    def arrived(i):
        d = peer(i)
        return pltpu.make_async_remote_copy(
            src_ref=grecv.at[d], dst_ref=grecv.at[d], send_sem=s2.at[d], recv_sem=r2.at[d],
            device_id=(k, d), device_id_type=MESH)

    for c in range(parts):
        def push(i):
            put_window(send, c, peer(i))
            chunk_copy(c, i).start()

        loop(push)
        put_window(recv, c, o)
    live = rows_ref[o]
    group = 4
    span = group * 2 * NX
    lane = lax.broadcasted_iota(jnp.int32, (count, span), 1)
    is_real = lax.rem(lane, 2 * NX) < NX

    def turned(x):
        return jnp.where(is_real, pltpu.roll(x, span - NX, 1), -pltpu.roll(x, NX, 1))

    def build(c, inner, carry):
        real, imag = carry
        g = c * (chunk // group) + inner
        lines = []
        for j in range(group):
            base = c * ranks * block + inner * group + j
            x3 = jnp.concatenate(
                [recv[pl.ds(base + t * chunk, ranks, stride=block), :] for t in range(lane_tiles)], axis=1
            )
            line = jnp.concatenate([x3[:, s * 2 * NX:(s + 1) * 2 * NX] for s in range(slots)], axis=0)
            lines.append(line)
        x = jnp.concatenate(lines, axis=1)
        x = jnp.where(lane // (2 * NX) + g * group < live, x, 0.0)
        flat[:, pl.ds(pl.multiple_of(g * span, 128), span)] = x
        xh, xl = split(x)
        th, tl = split(turned(x))
        real = real + dot_nt(xh, xh) + dot_nt(xh, xl) + dot_nt(xl, xh)
        imag = imag + dot_nt(xh, th) + dot_nt(xh, tl) + dot_nt(xl, th)
        return real, imag

    zero = jnp.zeros((count, count), jnp.float32)
    real = imag = zero
    for c in range(parts):
        loop(lambda i: chunk_arrived(c, i).wait_recv())
        real, imag = lax.fori_loop(0, chunk // group, functools.partial(build, c), (real, imag))
    ri = lax.broadcasted_iota(jnp.int32, (count, count), 0)
    ci = lax.broadcasted_iota(jnp.int32, (count, count), 1)
    packed = jnp.where(ri <= ci, real, imag)
    half = count // 2
    mine = jnp.concatenate([packed[:half], packed[half:]], axis=1)
    gsend[...] = mine
    grecv[o] = mine
    loop(lambda i: copy(i).start())
    loop(lambda i: arrived(i).wait_recv())
    total = grecv[0]
    for j in range(1, ranks):
        total = total + grecv[j]
    packed = jnp.concatenate([total[:, :count], total[:, count:]], axis=0)
    other = packed.T
    real = jnp.where(ri <= ci, packed, other)
    imag = jnp.where(ri > ci, packed, jnp.where(ri < ci, -other, 0.0))
    pick = pick_ref[...]
    exact = functools.partial(jnp.dot, precision=exact_mode, preferred_element_type=jnp.float32)
    real_picked = exact(pick, real)
    imag_picked = exact(pick, imag)
    diagonal = jnp.sum(jnp.where(ri == ci, real, 0.0), axis=1, keepdims=True)
    trace = jnp.sum(exact(pick, jnp.broadcast_to(diagonal, (count, 128)))[:, :1])
    components = rows * 2 * NX
    mean_square = trace / (orbs * components) + 1e-06
    shrink = 0.5 / (components * mean_square)
    norm = 1.0 / jnp.sqrt(jnp.full((1, 1), mean_square, jnp.float32))
    used = jnp.sum(pick, axis=0, keepdims=True)
    rot_real = (1.5 * pick - shrink * real_picked * used) * norm
    rot_imag = (shrink * imag_picked * used) * norm
    rh, rl = split(rot_real)
    ih, il = split(rot_imag)

    def rotate(g, c):
        at = pl.ds(pl.multiple_of(g * span, 128), span)
        x = flat[:, at]
        xh, xl = split(x)
        th, tl = split(turned(x))
        out_ref[:, at] = mm(rh, rl, xh, xl) - mm(ih, il, th, tl)
        return c

    lax.fori_loop(0, cap // group, rotate, 0)
    for c in range(parts):
        loop(lambda i: chunk_copy(c, i).wait_send())
    loop(lambda i: copy(i).wait_send())


def on_device(wavefunctions, kpoint_vector, kpoint_weight, occupation, orbital_slot, piece_rows,
              external_potential, core_density):
    f32 = jnp.float32
    slots = wavefunctions.shape[1]
    ranks = lax.axis_size("orb")
    kpts = lax.axis_size("kpt")
    orbs = orbital_slot.shape[0]
    rows = NZ * NY
    cap = 2 * rows // ranks
    width = slots * 2 * NX
    slab = external_potential.shape[1]
    lines = wavefunctions.reshape(slots * rows * 2 * NX // 128, 128)
    offsets = jnp.cumsum(piece_rows) - piece_rows
    place = (orbital_slot % slots) * ranks + orbital_slot // slots
    pick = (place[:, None] == jnp.arange(slots * ranks, dtype=jnp.int32)[None, :]).astype(f32)
    consts = tables()
    every = kpts * ranks
    planes = NZ // kpts
    lane_tiles = -(-width // 128)
    vm = pltpu.VMEM
    dma = pltpu.SemaphoreType.DMA
    density, filtered = pl.pallas_call(
        functools.partial(field_kernel, slots, kpts, ranks),
        out_shape=[jax.ShapeDtypeStruct((NZ, slab), f32), jax.ShapeDtypeStruct((rows, width), f32)],
        in_specs=[VMEM] * 3 + [SMEM] * 2 + [VMEM] * (2 + len(consts)), out_specs=[VMEM] * 2,
        scratch_shapes=[vm((lane_tiles * rows, 128), f32), vm((rows, width), f32),
                        vm((rows, width), f32), vm((NZ, NY * NX), f32), vm((rows, NX), f32),
                        vm((NZ, NY * NX), f32), vm((rows, NX), f32), vm((rows, width), f32)]
        + [vm((rows, rows), BF)] * 8 + [vm((width, width), BF)] * 6 + [vm((rows, width), BF)] * 8
        + [vm((every, planes, slab), f32)] * 2
        + [vm((planes, slab), f32), vm((every, planes, slab), f32),
           vm((planes, slab), f32), vm((kpts, planes, slab), f32)]
        + [dma((every,))] * 4 + [dma((kpts,))] * 2,
        compiler_params=pltpu.CompilerParams(collective_id=0, has_side_effects=True),
        name="field",
    )(lines, occupation[None], orbital_slot[None], kpoint_vector, kpoint_weight,
      external_potential, core_density, *consts)
    count = slots * ranks
    lane_tiles = -(-width // 128)
    new_rows = pl.pallas_call(
        functools.partial(exchange_kernel, slots, ranks, cap, orbs),
        out_shape=jax.ShapeDtypeStruct((orbs, cap * 2 * NX), f32),
        in_specs=[VMEM, SMEM, SMEM, VMEM], out_specs=VMEM,
        scratch_shapes=[pltpu.VMEM((lane_tiles * (rows + (cap + 15) // 8 * 8), 128), f32)]
        + [pltpu.VMEM((ranks * lane_tiles * cap, 128), f32)] * 2
        + [pltpu.VMEM((count, cap * 2 * NX), f32), pltpu.VMEM((count // 2, 2 * count), f32),
           pltpu.VMEM((ranks, count // 2, 2 * count), f32)] + [dma((CHUNKS * ranks,))] * 2
        + [dma((ranks,))] * 2,
        compiler_params=pltpu.CompilerParams(collective_id=1, has_side_effects=True),
        name="exchange",
    )(filtered, offsets, piece_rows, pick)
    return (density, new_rows[None])


def solution(mesh):
    in_specs = (
        P("kpt", "orb", None),
        P("kpt", None),
        P("kpt"),
        P(),
        P(),
        P(),
        P(None, "orb"),
        P(None, "orb"),
    )
    out_specs = (P(None, "orb"), P("kpt", None, "orb"))
    return jax.shard_map(
        on_device, mesh=mesh, in_specs=in_specs, out_specs=out_specs, check_vma=False
    )
```
